32 devices in a mesh: lat: 4 (over z), lon: 8 (over y, x, core).
Axes of the slice: x: 2, y: 2, z: 4, core: 2. Of those that a mesh axis runs over, the one named last changes fastest.
Arguments:
- samples: bfloat16 [256, 90112], P(None, ('lat', 'lon')), may hold values from -6 to 6
- area_weight: float32 [90112], P(('lat', 'lon')), may hold values from 0.1 to 1
- ocean_count: int32 [4, 8], P('lat', 'lon'), may hold values from 704 to 2816, as said below
- omega: bfloat16 [512, 256], replicated, may hold values from -5 to 5
Outputs:
- point_basis: bfloat16 [512, 90112], P(None, ('lat', 'lon'))
- sample_basis: float32 [8, 256, 64], replicated
The draws below stay inside these ranges and needn't reach their ends.
Inputs may be any that keep to these rules, and one draw needn't show every extreme that they name: Each device's block of grid points starts with ocean_count ocean points, the rest are land; some device's block is all ocean (2816).
All inputs are finite; a program needn't handle non-finite values.
Results may differ from the reference program's by a relative error of at most 0.0075.
Values sent between devices are 32-bit elements; how exact they have to be, the bound alone decides.
No kernel may reach another device: no remote copies, remote signals or barrier semaphores. Data moves between devices by JAX's collectives and lax.ppermute only.
A program may use at most 64 MiB of HBM per device.

```python
import math
import jax
import jax.numpy as jnp
from jax import lax

PTS_DEV = 2816
SAMPLES = 256
COLUMNS = 64
FOLDS = 8
BANDS = 4
SECTORS = 8
NPTS = 90112
N_LAT = 4
N_LON = 8


def draw_ocean_count(key, part):
    first = jax.random.fold_in(key, 11)
    second = jax.random.fold_in(key, 23)
    counts = jax.random.randint(first, (BANDS, SECTORS), PTS_DEV // 4, PTS_DEV + 1)
    picked = jax.random.randint(second, (), 0, BANDS * SECTORS)
    places = jnp.arange(BANDS * SECTORS, dtype=jnp.int32).reshape(BANDS, SECTORS)
    return jnp.where(places == picked, PTS_DEV, counts).astype(jnp.int32)


def levels(rng, shape, split, least, top_value):
    loudness = 1.0
    for position, blocks in split:
        draws = jax.random.uniform(jax.random.fold_in(jax.random.fold_in(rng, 6), position), (blocks,), jnp.float32, least / len(split), top_value / len(split))
        loudness = loudness * jnp.repeat(jnp.exp(draws), shape[position] // blocks).reshape((-1,) + (1,) * (len(shape) - 1 - position))
    return loudness


def bell_draw(own_key, extent, scale, limit, cuts=(), kind=jnp.bfloat16):
    values = scale * jax.random.normal(own_key, extent, jnp.float32)
    if cuts:
        values = values * levels(own_key, extent, cuts, -0.22, 0.18)
    return jnp.clip(values, -limit, limit).astype(kind)


def setup_inputs(seed: int = 0) -> dict:
    key_list = jax.random.split(jax.random.key(seed), 5)
    samples = bell_draw(key_list[0], (SAMPLES, NPTS), 1.0, 6.0, ((1, 32),))
    area_weight = jnp.clip(jnp.exp(math.log(1.0) - 2.3025851 * jax.random.uniform(key_list[1], (NPTS,), jnp.float32) ** levels(key_list[1], (NPTS,), ((0, 32),), -0.2, 0.2)), 0.1, 1.0)
    ocean_count = draw_ocean_count(jax.random.fold_in(key_list[4], 71), 0)
    omega = bell_draw(key_list[3], (FOLDS * COLUMNS, SAMPLES), 1.0, 5.0)
    return dict(samples=samples, area_weight=area_weight, ocean_count=ocean_count, omega=omega)


def held_out(omega_rows):
    fold_row = jnp.arange(FOLDS * COLUMNS, dtype=jnp.int32) // COLUMNS
    fold_col = jnp.arange(SAMPLES, dtype=jnp.int32) // (SAMPLES // FOLDS)
    keep = fold_row[:, None] != fold_col[None, :]
    return jnp.where(keep, omega_rows, jnp.zeros_like(omega_rows))

def block_data(samples, area_weight, counts_flat, live, index):
    start = (index * PTS_DEV).astype(jnp.int32)
    block = lax.dynamic_slice_in_dim(samples, start, PTS_DEV, 1)
    weights = lax.dynamic_slice_in_dim(area_weight, start, PTS_DEV, 0)
    valid = jnp.arange(PTS_DEV, dtype=jnp.int32) < counts_flat[index]
    weighted = jnp.where(valid[None, :], block.astype(jnp.float32) * weights[None, :], jnp.float32(0.0)).astype(jnp.bfloat16)
    product = jnp.dot(live.astype(jnp.float32), weighted.astype(jnp.float32), preferred_element_type=jnp.float32)
    return (weighted, product)

def reference(samples, area_weight, ocean_count, omega):
    blocks = N_LAT * N_LON
    counts_flat = ocean_count.reshape(-1).astype(jnp.int32)
    live = held_out(omega)

    def accumulate(carry, index):
        gram, cross = carry
        weighted, product = block_data(samples, area_weight, counts_flat, live, index)
        folded = product.reshape(FOLDS, COLUMNS, PTS_DEV)
        gram = gram + jnp.einsum('fkp,fjp->fkj', folded, folded, precision=lax.Precision.HIGHEST)
        cross = cross + jnp.einsum('sp,fkp->fsk', weighted.astype(jnp.float32), folded, precision=lax.Precision.HIGHEST)
        return ((gram, cross), None)
    start_carry = (jnp.zeros((FOLDS, COLUMNS, COLUMNS), jnp.float32), jnp.zeros((FOLDS, SAMPLES, COLUMNS), jnp.float32))
    (gram, cross), _ = lax.scan(accumulate, start_carry, jnp.arange(blocks, dtype=jnp.int32))
    factor = jnp.linalg.cholesky(gram)
    identity = jnp.broadcast_to(jnp.eye(COLUMNS, dtype=jnp.float32), (FOLDS, COLUMNS, COLUMNS))
    inverse = jax.scipy.linalg.solve_triangular(factor, identity, lower=True)
    total = PTS_DEV * blocks
    point_scale = (inverse * jnp.float32(total ** 0.5)).astype(jnp.bfloat16)

    def project(index):
        _, product = block_data(samples, area_weight, counts_flat, live, index)
        scores = product.astype(jnp.bfloat16)
        folded = scores.reshape(FOLDS, COLUMNS, PTS_DEV).astype(jnp.float32)
        result = jnp.einsum('fkj,fjp->fkp', point_scale.astype(jnp.float32), folded)
        return result.astype(jnp.bfloat16).reshape(FOLDS * COLUMNS, PTS_DEV)
    pieces = lax.map(project, jnp.arange(blocks, dtype=jnp.int32))
    point_basis = jnp.transpose(pieces, (1, 0, 2)).reshape(FOLDS * COLUMNS, total)
    sample_scale = inverse * jnp.float32((SAMPLES / total) ** 0.5)
    sample_basis = jnp.einsum('fsj,fkj->fsk', cross, sample_scale, precision=lax.Precision.HIGHEST)
    return (point_basis, sample_basis)
```

```python
import jax
import jax.numpy as jnp
from jax import lax
from jax.sharding import PartitionSpec as P

SAMPLES = 256
COLUMNS = 64
FOLDS = 8
AXES = ("lat", "lon")


def grid_total(value):
    lon = lax.axis_size("lon")
    devices = lax.axis_size("lat") * lon
    if devices & (devices - 1):
        return lax.psum(value, AXES)
    bit = 1
    while bit < devices:
        pairs = [(d, d ^ bit) for d in range(devices)]
        value = value + lax.ppermute(value, AXES, pairs)
        bit *= 2
    return value


def on_device(samples, area_weight, ocean_count, omega):
    point_cols = samples.shape[1]
    fold_row = lax.iota(jnp.int32, FOLDS * COLUMNS) // COLUMNS
    fold_col = lax.iota(jnp.int32, SAMPLES) // (SAMPLES // FOLDS)
    keeping = fold_row[:, None] != fold_col[None, :]
    live = jnp.where(keeping, omega, jnp.zeros_like(omega))
    valid = lax.iota(jnp.int32, point_cols) < ocean_count[0, 0]
    weighted = jnp.where(
        valid[None, :], samples.astype(jnp.float32) * area_weight[None, :], jnp.float32(0.0)
    ).astype(jnp.bfloat16)
    partial_cov = jnp.einsum("sp,tp->st", weighted, weighted, preferred_element_type=jnp.float32)
    cov = grid_total(partial_cov)
    product = jnp.dot(live, weighted, preferred_element_type=jnp.float32)
    scores = product.astype(jnp.bfloat16)
    folded = scores.reshape(FOLDS, COLUMNS, point_cols)
    devices_all = lax.axis_size("lat") * lax.axis_size("lon")
    total = point_cols * devices_all
    live_f = live.astype(jnp.float32).reshape(FOLDS, COLUMNS, SAMPLES)
    cross = jnp.einsum("st,fkt->fsk", cov, live_f, precision=lax.Precision.HIGHEST)
    gram = jnp.einsum("fks,fsj->fkj", live_f, cross, precision=lax.Precision.HIGHEST)
    lower_factor = jnp.linalg.cholesky(gram)
    identity = jnp.broadcast_to(jnp.eye(COLUMNS, dtype=jnp.float32), (FOLDS, COLUMNS, COLUMNS))
    inverse = jax.scipy.linalg.solve_triangular(lower_factor, identity, lower=True)
    point_scale = (inverse * jnp.float32(total**0.5)).astype(jnp.bfloat16)
    point_basis = jnp.einsum(
        "fkj,fjp->fkp", point_scale, folded, preferred_element_type=jnp.float32
    )
    point_basis = point_basis.astype(jnp.bfloat16).reshape(FOLDS * COLUMNS, point_cols)
    sample_scale = inverse * jnp.float32((SAMPLES / total) ** 0.5)
    sample_basis = jnp.einsum("fsj,fkj->fsk", cross, sample_scale, precision=lax.Precision.HIGHEST)
    return (point_basis, sample_basis)


def solution(mesh):
    in_specs = (P(None, AXES), P(AXES), P("lat", "lon"), P())
    out_specs = (P(None, AXES), P())
    return jax.shard_map(
        on_device, mesh=mesh, in_specs=in_specs, out_specs=out_specs, check_vma=False
    )
```

```python
import jax
import jax.numpy as jnp
from jax import lax
from jax.experimental import pallas as pl
from jax.experimental.pallas import tpu as pltpu
from jax.sharding import PartitionSpec as P

SAMPLES = 256
COLUMNS = 64
FOLDS = 8
AXES = ("lat", "lon")
HALF = SAMPLES // 2
QUARTER = HALF // 2
PACKED = 2 * QUARTER + 8
BLOCK = 8
WIDE = 4 * COLUMNS
NT = (((1,), (1,)), ((), ()))
VMEM = pltpu.VMEM
SPLIT = 3


def iota(shape, dim):
    return lax.broadcasted_iota(jnp.int32, shape, dim)


def split_bf16(value):
    parts = []
    for _ in range(SPLIT):
        part = value.astype(jnp.bfloat16)
        parts.append(part)
        value = value - part.astype(jnp.float32)
    return parts


def dot_nt(a, b):
    return lax.dot_general(a, b, NT, preferred_element_type=jnp.float32)


def chunks_of(cols, width):
    return [(start, min(width, cols - start)) for start in range(0, cols, width)]


def cov_kernel(scalars, samples, area, weighted, mine, other, held, sems):
    cols = area.shape[1]
    parts = chunks_of(cols, 768)
    copies = []
    for n, (start, width) in enumerate(parts):
        copies.append(
            pltpu.make_async_copy(
                samples.at[:, pl.ds(start, width)], held.at[:, pl.ds(start, width)], sems.at[n]
            )
        )
        copies[-1].start()
    masked = jnp.where(iota((1, cols), 1) < scalars[0], area[...], 0.0)
    cov = jnp.zeros((SAMPLES, SAMPLES), jnp.float32)
    for copy, (start, width) in zip(copies, parts):
        copy.wait()
        part = held[:, start : start + width].astype(jnp.float32) * masked[:, start : start + width]
        part = part.astype(jnp.bfloat16)
        weighted[:, start : start + width] = part
        cov = cov + dot_nt(part, part)
    row, col = iota((HALF, HALF), 0), iota((HALF, HALF), 1)
    last = cov[HALF:, HALF:]
    diagonal = jnp.sum(jnp.where(row == col, last, 0.0), axis=0, keepdims=True)
    diagonal = jnp.broadcast_to(diagonal, (8, HALF))
    triangles = jnp.where(row >= col, cov[:HALF, :HALF], last)
    square = cov[:HALF, HALF:]
    first = scalars[1] == 0
    for ref, low in ((mine, first), (other, jnp.logical_not(first))):
        ref[:QUARTER] = jnp.where(low, triangles[:QUARTER], triangles[QUARTER:])
        ref[QUARTER:HALF] = jnp.where(low, square[:QUARTER], square[QUARTER:])
        ref[HALF:] = diagonal


def lane(value, i):
    return jnp.broadcast_to(value[:, i : i + 1], value.shape)


def eliminate(rows):
    for j in range(0, COLUMNS, BLOCK):
        pivots = [rows[j + q] for q in range(BLOCK)]
        near = range(j, min(j + 2 * BLOCK, COLUMNS))
        coef = [{i: lane(pivots[q], i) for i in near if i >= j + q} for q in range(BLOCK)]
        done = []
        for q in range(BLOCK):
            scale = lax.rsqrt(coef[q][j + q])
            done.append(pivots[q] * scale)
            for i in coef[q]:
                coef[q][i] = coef[q][i] * scale
            for r in range(q + 1, BLOCK):
                pivots[r] = pivots[r] - coef[q][j + r] * done[q]
                for i in coef[r]:
                    coef[r][i] = coef[r][i] - coef[q][j + r] * coef[q][i]
        for q in range(BLOCK):
            rows[j + q] = done[q]
        for i in range(j + BLOCK, COLUMNS):
            value = rows[i]
            for q in range(BLOCK):
                value = value - (coef[q][i] if i in coef[q] else lane(done[q], i)) * done[q]
            rows[i] = value


def finish_kernel(total, scalars, mine, other, live, scores, basis, sample_basis,
                  rows, diag, scores_v, basis_v, sample_v, sems):
    cols = scores.shape[1]
    fetch = pltpu.make_async_copy(scores, scores_v, sems.at[0])
    fetch.start()
    diag[...] = jnp.zeros_like(diag)

    first = scalars[1] == 0
    low = jnp.where(first, mine[...], other[...])
    high = jnp.where(first, other[...], mine[...])
    triangles = jnp.concatenate([low[:QUARTER], high[:QUARTER]], axis=0)
    square = jnp.concatenate([low[QUARTER:HALF], high[QUARTER:HALF]], axis=0)
    row, col = iota((HALF, HALF), 0), iota((HALF, HALF), 1)
    flipped = triangles.T
    upper = jnp.where(row >= col, triangles, flipped)
    lower = jnp.where(row < col, triangles, flipped)
    lower = jnp.where(row == col, jnp.broadcast_to(low[HALF : HALF + 1], (HALF, HALF)), lower)
    cov = jnp.concatenate(
        [
            jnp.concatenate([upper, square], axis=1),
            jnp.concatenate([square.T, lower], axis=1),
        ],
        axis=0,
    )
    cov_parts = split_bf16(cov)
    test = live[...]
    mixed = jnp.zeros((FOLDS * COLUMNS, SAMPLES), jnp.float32)
    for part in cov_parts:
        mixed = mixed + jnp.dot(test, part, preferred_element_type=jnp.float32)
    eye = (iota((COLUMNS, COLUMNS), 0) == iota((COLUMNS, COLUMNS), 1)).astype(jnp.float32)
    for f in range(FOLDS):
        own = slice(f * COLUMNS, (f + 1) * COLUMNS)
        gram = jnp.zeros((COLUMNS, COLUMNS), jnp.float32)
        for part in split_bf16(mixed[own]):
            gram = gram + dot_nt(part, test[own])
        rows[:, f, :] = jnp.concatenate([gram, eye], axis=1)

    eliminate(rows)

    in_low = iota((COLUMNS, 2 * COLUMNS), 1) < COLUMNS
    for f in range(FOLDS):
        inverse = rows[:, f, :]
        if f % 2 == 0:
            inverse = jnp.where(in_low, pltpu.roll(inverse, COLUMNS, 1), 0.0)
        else:
            inverse = jnp.where(in_low, 0.0, inverse)
        at = (f % 4) // 2 * 2 * COLUMNS
        diag[f * COLUMNS : (f + 1) * COLUMNS, at : at + 2 * COLUMNS] = inverse

    fetch.wait()
    copies = []
    for g in range(FOLDS // 4):
        own = slice(g * WIDE, (g + 1) * WIDE)
        scale = (diag[own] * jnp.float32(total**0.5)).astype(jnp.bfloat16)
        for n, (start, width) in enumerate(chunks_of(cols, 768)):
            at = slice(start, start + width)
            basis_v[own, at] = jnp.dot(
                scale, scores_v[own, at], preferred_element_type=jnp.float32
            ).astype(jnp.bfloat16)
            where = (pl.ds(g * WIDE, WIDE), pl.ds(start, width))
            copies.append(
                pltpu.make_async_copy(basis_v.at[where], basis.at[where], sems.at[1 + len(copies)])
            )
            copies[-1].start()
    for g in range(FOLDS // 4):
        own = slice(g * WIDE, (g + 1) * WIDE)
        sample_v[own] = jnp.dot(
            diag[own] * jnp.float32((SAMPLES / total) ** 0.5), mixed[own],
            precision=lax.Precision.HIGHEST, preferred_element_type=jnp.float32,
        )
        where = pl.ds(g * WIDE, WIDE)
        copies.append(
            pltpu.make_async_copy(
                sample_v.at[where], sample_basis.at[where], sems.at[1 + len(copies)]
            )
        )
        copies[-1].start()
    for copy in copies:
        copy.wait()


def spec(space):
    return pl.BlockSpec(memory_space=space)


def grid_total(mine, other):
    devices = lax.axis_size("lat") * lax.axis_size("lon")
    bits = []
    while 2 << len(bits) < devices:
        bits.append(2 << len(bits))
    assert devices == 2 << len(bits)
    near, far = bits[: len(bits) // 2], bits[len(bits) // 2 :]
    order = [bit for pair in zip(near, far) for bit in pair] + far[len(near) :]
    swap = [bit for pair in zip(far, near) for bit in pair] + far[len(near) :]
    total = mine + lax.ppermute(other, AXES, [(d, d ^ 1) for d in range(devices)])
    for bit in zip(order, swap):
        pairs = [(d, d ^ bit[d % 2]) for d in range(devices)]
        total = total + lax.ppermute(total, AXES, pairs)
    return total, lax.ppermute(total, AXES, [(d, d ^ 1) for d in range(devices)])


def on_device(samples, area_weight, ocean_count, omega):
    cols = samples.shape[1]
    total = cols * lax.axis_size("lat") * lax.axis_size("lon")
    core = lax.axis_index("lon") % 2
    scalars = jnp.stack([ocean_count[0, 0], core])
    half = jax.ShapeDtypeStruct((PACKED, HALF), jnp.float32)
    weighted, mine, other = pl.pallas_call(
        cov_kernel,
        out_shape=(jax.ShapeDtypeStruct((SAMPLES, cols), jnp.bfloat16), half, half),
        in_specs=[spec(pltpu.SMEM), spec(pl.ANY), spec(VMEM)],
        out_specs=(spec(VMEM), spec(VMEM), spec(VMEM)),
        scratch_shapes=[VMEM((SAMPLES, cols), jnp.bfloat16), pltpu.SemaphoreType.DMA((8,))],
        cost_estimate=pl.CostEstimate(
            flops=2 * SAMPLES * SAMPLES * cols, bytes_accessed=4 * SAMPLES * cols, transcendentals=0
        ),
        compiler_params=pltpu.CompilerParams(vmem_limit_bytes=16 << 20),
        name="cov",
    )(scalars, samples, area_weight.reshape(1, cols))

    mine, other = grid_total(mine, other)

    fold_row = lax.iota(jnp.int32, FOLDS * COLUMNS) // COLUMNS
    fold_col = lax.iota(jnp.int32, SAMPLES) // (SAMPLES // FOLDS)
    keeping = fold_row[:, None] != fold_col[None, :]
    live = jnp.where(keeping, omega, jnp.zeros_like(omega))
    product = jnp.dot(live, weighted, preferred_element_type=jnp.float32)
    scores = product.astype(jnp.bfloat16)

    point_basis, sample_basis = pl.pallas_call(
        lambda *refs: finish_kernel(total, *refs),
        out_shape=(
            jax.ShapeDtypeStruct((FOLDS * COLUMNS, cols), jnp.bfloat16),
            jax.ShapeDtypeStruct((FOLDS * COLUMNS, SAMPLES), jnp.float32),
        ),
        in_specs=[spec(pltpu.SMEM), spec(VMEM), spec(VMEM), spec(VMEM), spec(pl.ANY)],
        out_specs=(spec(pl.ANY), spec(pl.ANY)),
        scratch_shapes=[
            VMEM((COLUMNS, FOLDS, 2 * COLUMNS), jnp.float32),
            VMEM((FOLDS * COLUMNS, WIDE), jnp.float32),
            VMEM((FOLDS * COLUMNS, cols), jnp.bfloat16),
            VMEM((FOLDS * COLUMNS, cols), jnp.bfloat16),
            VMEM((FOLDS * COLUMNS, SAMPLES), jnp.float32),
            pltpu.SemaphoreType.DMA((16,)),
        ],
        compiler_params=pltpu.CompilerParams(vmem_limit_bytes=16 << 20),
        name="finish",
    )(scalars, mine, other, live, scores)
    sample_basis = sample_basis.reshape(FOLDS, COLUMNS, SAMPLES)
    return point_basis, sample_basis.transpose(0, 2, 1)


def solution(mesh):
    in_specs = (P(None, AXES), P(AXES), P("lat", "lon"), P())
    out_specs = (P(None, AXES), P())
    return jax.shard_map(
        on_device, mesh=mesh, in_specs=in_specs, out_specs=out_specs, check_vma=False
    )
```

```python
import jax
import jax.numpy as jnp
from jax import lax
from jax.experimental import pallas as pl
from jax.experimental.pallas import tpu as pltpu
from jax.sharding import PartitionSpec as P

SAMPLES = 256
COLUMNS = 64
FOLDS = 8
AXES = ("lat", "lon")
HALF = SAMPLES // 2
QUARTER = HALF // 2
PACKED = 2 * QUARTER + 8
BLOCK = 8
WIDE = 4 * COLUMNS
NT = (((1,), (1,)), ((), ()))
VMEM = pltpu.VMEM
SPLIT = 3


def iota(shape, dim):
    return lax.broadcasted_iota(jnp.int32, shape, dim)


def split_bf16(value):
    parts = []
    for _ in range(SPLIT):
        part = value.astype(jnp.bfloat16)
        parts.append(part)
        value = value - part.astype(jnp.float32)
    return parts


def dot_nt(a, b):
    return lax.dot_general(a, b, NT, preferred_element_type=jnp.float32)


def chunks_of(cols, width):
    return [(start, min(width, cols - start)) for start in range(0, cols, width)]


def cov_kernel(count, samples, area, weighted, mine, other, held, area_v, sems):
    cols = samples.shape[1]
    parts = chunks_of(cols, 768)
    fetch = pltpu.make_async_copy(area, area_v.at[0], sems.at[len(parts)])
    fetch.start()
    copies = []
    for n, (start, width) in enumerate(parts):
        copies.append(
            pltpu.make_async_copy(
                samples.at[:, pl.ds(start, width)], held.at[:, pl.ds(start, width)], sems.at[n]
            )
        )
        copies[-1].start()
    fetch.wait()
    masked = jnp.where(iota((1, cols), 1) < count[0, 0], area_v[...], 0.0)
    cov = jnp.zeros((SAMPLES, SAMPLES), jnp.float32)
    for copy, (start, width) in zip(copies, parts):
        copy.wait()
        part = held[:, start : start + width].astype(jnp.float32) * masked[:, start : start + width]
        part = part.astype(jnp.bfloat16)
        weighted[:, start : start + width] = part
        cov = cov + dot_nt(part, part)
    row, col = iota((HALF, HALF), 0), iota((HALF, HALF), 1)
    last = cov[HALF:, HALF:]
    diagonal = jnp.sum(jnp.where(row == col, last, 0.0), axis=0, keepdims=True)
    diagonal = jnp.broadcast_to(diagonal, (8, HALF))
    triangles = jnp.where(row >= col, cov[:HALF, :HALF], last)
    square = cov[:HALF, HALF:]
    first = lax.axis_index("lon") % 2 == 0
    for ref, low in ((mine, first), (other, jnp.logical_not(first))):
        ref[:QUARTER] = jnp.where(low, triangles[:QUARTER], triangles[QUARTER:])
        ref[QUARTER:HALF] = jnp.where(low, square[:QUARTER], square[QUARTER:])
        ref[HALF:] = diagonal


def lane(value, i):
    return jnp.broadcast_to(value[:, i : i + 1], value.shape)


def take(value, index):
    return jnp.take_along_axis(value, index, axis=1, mode="promise_in_bounds")


def eliminate(rows):
    at = iota((FOLDS, 2 * COLUMNS), 1)
    even = at < COLUMNS
    column = jnp.where(even, at, at - COLUMNS)
    odd = jnp.where(even, 0, 1)
    for j in range(0, COLUMNS, BLOCK):
        raw = []
        for p in range(j // 2, (j + BLOCK) // 2):
            pair = rows[p]
            swapped = pltpu.roll(pair, COLUMNS, 1)
            raw += [jnp.where(even, pair, swapped), jnp.where(even, swapped, pair)]
        near = range((j + BLOCK) // 2, min(j // 2 + BLOCK, COLUMNS // 2))
        coef = [{r: lane(raw[q], j + r) for r in range(q, BLOCK)} for q in range(BLOCK)]
        pairs = [{p: take(raw[q], odd + 2 * p) for p in near} for q in range(BLOCK)]
        inside = (column >= j) & (column < j + BLOCK)
        pivots = [jnp.where(inside, 0.0, value) for value in raw]
        done = []
        for q in range(BLOCK):
            scale = lax.rsqrt(coef[q][q])
            done.append(jnp.where(column == j + q, scale, pivots[q] * scale))
            for have in (coef[q], pairs[q]):
                for i in have:
                    have[i] = have[i] * scale
            for r in range(q + 1, BLOCK):
                factor = coef[q][r]
                pivots[r] = pivots[r] - factor * done[q]
                for have, used in ((coef, coef[r]), (pairs, pairs[r])):
                    for i in used:
                        used[i] = used[i] - factor * have[q][i]
        for q in range(0, BLOCK, 2):
            rows[(j + q) // 2] = jnp.where(even, done[q], done[q + 1])
        for p in range((j + BLOCK) // 2, COLUMNS // 2):
            value = jnp.where(inside, 0.0, rows[p])
            for q in range(BLOCK):
                factor = pairs[q][p] if p in near else take(done[q], odd + 2 * p)
                value = value - factor * done[q]
            rows[p] = value


def beside(ref, rows):
    return jnp.concatenate([ref[0, rows, :], ref[1, rows, :]], axis=1)


def finish_kernel(total, mine, other, live, scores, basis, sample_basis,
                  rows, diag, mixed_v, basis_v, sample_v, sems):
    cols = scores.shape[1]
    diag[...] = jnp.zeros_like(diag)

    first = lax.axis_index("lon") % 2 == 0
    low = jnp.where(first, mine[...], other[...])
    high = jnp.where(first, other[...], mine[...])
    triangles = jnp.concatenate([low[:QUARTER], high[:QUARTER]], axis=0)
    square = jnp.concatenate([low[QUARTER:HALF], high[QUARTER:HALF]], axis=0)
    row, col = iota((HALF, HALF), 0), iota((HALF, HALF), 1)
    flipped = triangles.T
    upper = jnp.where(row >= col, triangles, flipped)
    lower = jnp.where(row < col, triangles, flipped)
    lower = jnp.where(row == col, jnp.broadcast_to(low[HALF : HALF + 1], (HALF, HALF)), lower)
    cov = jnp.concatenate(
        [
            jnp.concatenate([upper, square], axis=1),
            jnp.concatenate([square.T, lower], axis=1),
        ],
        axis=0,
    )
    cov_parts = split_bf16(cov)
    test = live[...]
    mixed = jnp.zeros((FOLDS * COLUMNS, SAMPLES), jnp.float32)
    for part in cov_parts:
        mixed = mixed + jnp.dot(test, part, preferred_element_type=jnp.float32)
    for c in (0, 1):
        mixed_v[c] = mixed[:, c * HALF : (c + 1) * HALF]
    pairs = COLUMNS // 2
    for f in range(FOLDS):
        even, odd = (
            beside(mixed_v, pl.ds(f * COLUMNS + o, pairs, stride=2)) for o in (0, 1)
        )
        own = test[f * COLUMNS : (f + 1) * COLUMNS]
        gram = jnp.zeros((COLUMNS, COLUMNS), jnp.float32)
        for part in split_bf16(jnp.concatenate([even, odd], axis=0)):
            gram = gram + dot_nt(part, own)
        rows[:, f, :] = jnp.concatenate([gram[:pairs], gram[pairs:]], axis=1)

    eliminate(rows)

    at, pair = iota((pairs, 2 * COLUMNS), 1), iota((pairs, 2 * COLUMNS), 0)
    for f in range(FOLDS):
        left = f % 2 == 0
        found = rows[:, f, :]
        swapped = pltpu.roll(found, COLUMNS, 1)
        column = at if left else at - COLUMNS
        for o in (0, 1):
            keep = (column >= 0) & (column <= 2 * pair + o)
            value = jnp.where(keep, found if left == (o == 0) else swapped, 0.0)
            diag[f % 4 // 2, pl.ds(f * COLUMNS + o, pairs, stride=2), :] = value

    copies = []
    for g in range(FOLDS // 4):
        own = slice(g * WIDE, (g + 1) * WIDE)
        scale = (beside(diag, own) * jnp.float32(total**0.5)).astype(jnp.bfloat16)
        for n, (start, width) in enumerate(chunks_of(cols, 768)):
            at = slice(start, start + width)
            basis_v[own, at] = jnp.dot(
                scale, scores[own, at], preferred_element_type=jnp.float32
            ).astype(jnp.bfloat16)
            where = (pl.ds(g * WIDE, WIDE), pl.ds(start, width))
            copies.append(
                pltpu.make_async_copy(basis_v.at[where], basis.at[where], sems.at[len(copies)])
            )
            copies[-1].start()
    for g in range(FOLDS // 4):
        own = slice(g * WIDE, (g + 1) * WIDE)
        sample_v[own] = jnp.dot(
            beside(diag, own) * jnp.float32((SAMPLES / total) ** 0.5), beside(mixed_v, own),
            precision=lax.Precision.HIGHEST, preferred_element_type=jnp.float32,
        )
        where = pl.ds(g * WIDE, WIDE)
        copies.append(
            pltpu.make_async_copy(
                sample_v.at[where], sample_basis.at[where], sems.at[len(copies)]
            )
        )
        copies[-1].start()
    for copy in copies:
        copy.wait()


def spec(space):
    return pl.BlockSpec(memory_space=space)


def grid_total(mine, other):
    devices = lax.axis_size("lat") * lax.axis_size("lon")
    bits = []
    while 2 << len(bits) < devices:
        bits.append(2 << len(bits))
    assert devices == 2 << len(bits)
    near, far = bits[: len(bits) // 2], bits[len(bits) // 2 :]
    order = [bit for pair in zip(near, far) for bit in pair] + far[len(near) :]
    swap = [bit for pair in zip(far, near) for bit in pair] + far[len(near) :]
    total = mine + lax.ppermute(other, AXES, [(d, d ^ 1) for d in range(devices)])
    for bit in zip(order, swap):
        pairs = [(d, d ^ bit[d % 2]) for d in range(devices)]
        total = total + lax.ppermute(total, AXES, pairs)
    return total, lax.ppermute(total, AXES, [(d, d ^ 1) for d in range(devices)])


def on_device(samples, area_weight, ocean_count, omega):
    cols = samples.shape[1]
    total = cols * lax.axis_size("lat") * lax.axis_size("lon")
    half = jax.ShapeDtypeStruct((PACKED, HALF), jnp.float32)
    weighted, mine, other = pl.pallas_call(
        cov_kernel,
        out_shape=(jax.ShapeDtypeStruct((SAMPLES, cols), jnp.bfloat16), half, half),
        in_specs=[spec(pltpu.SMEM), spec(pltpu.HBM), spec(pltpu.HBM)],
        out_specs=(spec(VMEM), spec(VMEM), spec(VMEM)),
        scratch_shapes=[
            VMEM((SAMPLES, cols), jnp.bfloat16),
            VMEM((1, cols), jnp.float32),
            pltpu.SemaphoreType.DMA((8,)),
        ],
        cost_estimate=pl.CostEstimate(
            flops=2 * SAMPLES * SAMPLES * cols, bytes_accessed=4 * SAMPLES * cols, transcendentals=0
        ),
        compiler_params=pltpu.CompilerParams(vmem_limit_bytes=16 << 20),
        name="cov",
    )(
        ocean_count,
        pltpu.with_memory_space_constraint(samples, pltpu.HBM),
        pltpu.with_memory_space_constraint(area_weight, pltpu.HBM),
    )

    mine, other = grid_total(mine, other)

    fold_row = lax.iota(jnp.int32, FOLDS * COLUMNS) // COLUMNS
    fold_col = lax.iota(jnp.int32, SAMPLES) // (SAMPLES // FOLDS)
    keeping = fold_row[:, None] != fold_col[None, :]
    live = jnp.where(keeping, omega, jnp.zeros_like(omega))
    product = jnp.dot(live, weighted, preferred_element_type=jnp.float32)
    scores = product.astype(jnp.bfloat16)

    point_basis, sample_basis = pl.pallas_call(
        lambda *refs: finish_kernel(total, *refs),
        out_shape=(
            jax.ShapeDtypeStruct((FOLDS * COLUMNS, cols), jnp.bfloat16),
            jax.ShapeDtypeStruct((FOLDS * COLUMNS, SAMPLES), jnp.float32),
        ),
        in_specs=[spec(VMEM)] * 4,
        out_specs=(spec(pl.ANY), spec(pl.ANY)),
        scratch_shapes=[
            VMEM((COLUMNS // 2, FOLDS, 2 * COLUMNS), jnp.float32),
            VMEM((2, FOLDS * COLUMNS, WIDE // 2), jnp.float32),
            VMEM((2, FOLDS * COLUMNS, HALF), jnp.float32),
            VMEM((FOLDS * COLUMNS, cols), jnp.bfloat16),
            VMEM((FOLDS * COLUMNS, SAMPLES), jnp.float32),
            pltpu.SemaphoreType.DMA((16,)),
        ],
        compiler_params=pltpu.CompilerParams(vmem_limit_bytes=16 << 20),
        name="finish",
    )(mine, other, live, scores)
    sample_basis = sample_basis.reshape(FOLDS, COLUMNS, SAMPLES)
    return point_basis, sample_basis.transpose(0, 2, 1)


def solution(mesh):
    in_specs = (P(None, AXES), P(AXES), P("lat", "lon"), P())
    out_specs = (P(None, AXES), P())
    return jax.shard_map(
        on_device, mesh=mesh, in_specs=in_specs, out_specs=out_specs, check_vma=False
    )
```

```python
import jax
import jax.numpy as jnp
from jax import lax
from jax.experimental import pallas as pl
from jax.experimental.pallas import tpu as pltpu
from jax.sharding import PartitionSpec as P

SAMPLES = 256
COLUMNS = 64
FOLDS = 8
AXES = ("lat", "lon")
HALF = SAMPLES // 2
QUARTER = HALF // 2
PACKED = 2 * QUARTER + 8
BLOCK = 8
WIDE = 4 * COLUMNS
NT = (((1,), (1,)), ((), ()))
VMEM = pltpu.VMEM
SPLIT = 3


def iota(shape, dim):
    return lax.broadcasted_iota(jnp.int32, shape, dim)


def split_bf16(value):
    parts = []
    for _ in range(SPLIT):
        part = value.astype(jnp.bfloat16)
        parts.append(part)
        value = value - part.astype(jnp.float32)
    return parts


def dot_nt(a, b):
    return lax.dot_general(a, b, NT, preferred_element_type=jnp.float32)


def chunks_of(cols, width):
    return [(start, min(width, cols - start)) for start in range(0, cols, width)]


def cov_kernel(count, samples, area, weighted, mine, other, held, area_v, sems):
    cols = samples.shape[1]
    parts = chunks_of(cols, 1408)
    fetch = pltpu.make_async_copy(area, area_v.at[0], sems.at[len(parts)])
    fetch.start()
    copies = []
    for n, (start, width) in enumerate(parts):
        copies.append(
            pltpu.make_async_copy(
                samples.at[:, pl.ds(start, width)], held.at[:, pl.ds(start, width)], sems.at[n]
            )
        )
        copies[-1].start()
    fetch.wait()
    masked = jnp.where(iota((1, cols), 1) < count[0, 0], area_v[...], 0.0)
    cov = jnp.zeros((SAMPLES, SAMPLES), jnp.float32)
    for copy, (start, width) in zip(copies, parts):
        copy.wait()
        part = held[:, start : start + width].astype(jnp.float32) * masked[:, start : start + width]
        part = part.astype(jnp.bfloat16)
        weighted[:, start : start + width] = part
        cov = cov + dot_nt(part, part)
    row, col = iota((HALF, HALF), 0), iota((HALF, HALF), 1)
    last = cov[HALF:, HALF:]
    diagonal = jnp.sum(jnp.where(row == col, last, 0.0), axis=0, keepdims=True)
    diagonal = jnp.broadcast_to(diagonal, (8, HALF))
    triangles = jnp.where(row >= col, cov[:HALF, :HALF], last)
    square = cov[:HALF, HALF:]
    first = lax.axis_index("lon") % 2 == 0
    for ref, low in ((mine, first), (other, jnp.logical_not(first))):
        ref[:QUARTER] = jnp.where(low, triangles[:QUARTER], triangles[QUARTER:])
        ref[QUARTER:HALF] = jnp.where(low, square[:QUARTER], square[QUARTER:])
        ref[HALF:] = diagonal


def lane(value, i):
    return jnp.broadcast_to(value[:, i : i + 1], value.shape)


def take(value, index):
    return jnp.take_along_axis(value, index, axis=1, mode="promise_in_bounds")


def eliminate(rows):
    at = iota((FOLDS, 2 * COLUMNS), 1)
    even = at < COLUMNS
    column = jnp.where(even, at, at - COLUMNS)
    odd = jnp.where(even, 0, 1)
    for j in range(0, COLUMNS, BLOCK):
        raw = []
        for p in range(j // 2, (j + BLOCK) // 2):
            pair = rows[p]
            swapped = pltpu.roll(pair, COLUMNS, 1)
            raw += [jnp.where(even, pair, swapped), jnp.where(even, swapped, pair)]
        near = range((j + BLOCK) // 2, min(j // 2 + BLOCK, COLUMNS // 2))
        coef = [{r: lane(raw[q], j + r) for r in range(q, BLOCK)} for q in range(BLOCK)]
        pairs = [{p: take(raw[q], odd + 2 * p) for p in near} for q in range(BLOCK)]
        inside = (column >= j) & (column < j + BLOCK)
        pivots = [jnp.where(inside, 0.0, value) for value in raw]
        done = []
        for q in range(BLOCK):
            scale = lax.rsqrt(coef[q][q])
            done.append(jnp.where(column == j + q, scale, pivots[q] * scale))
            for have in (coef[q], pairs[q]):
                for i in have:
                    have[i] = have[i] * scale
            for r in range(q + 1, BLOCK):
                factor = coef[q][r]
                pivots[r] = pivots[r] - factor * done[q]
                for have, used in ((coef, coef[r]), (pairs, pairs[r])):
                    for i in used:
                        used[i] = used[i] - factor * have[q][i]
        for q in range(0, BLOCK, 2):
            rows[(j + q) // 2] = jnp.where(even, done[q], done[q + 1])
        for p in range((j + BLOCK) // 2, COLUMNS // 2):
            value = jnp.where(inside, 0.0, rows[p])
            for q in range(BLOCK):
                factor = pairs[q][p] if p in near else take(done[q], odd + 2 * p)
                value = value - factor * done[q]
            rows[p] = value


def beside(ref, rows):
    return jnp.concatenate([ref[0, rows, :], ref[1, rows, :]], axis=1)


def finish_kernel(total, mine, other, live, scores, basis, sample_basis,
                  rows, diag, mixed_v, basis_v, sample_v, sems):
    cols = scores.shape[1]
    diag[...] = jnp.zeros_like(diag)

    first = lax.axis_index("lon") % 2 == 0
    low = jnp.where(first, mine[...], other[...])
    high = jnp.where(first, other[...], mine[...])
    triangles = jnp.concatenate([low[:QUARTER], high[:QUARTER]], axis=0)
    square = jnp.concatenate([low[QUARTER:HALF], high[QUARTER:HALF]], axis=0)
    row, col = iota((HALF, HALF), 0), iota((HALF, HALF), 1)
    flipped = triangles.T
    upper = jnp.where(row >= col, triangles, flipped)
    lower = jnp.where(row < col, triangles, flipped)
    lower = jnp.where(row == col, jnp.broadcast_to(low[HALF : HALF + 1], (HALF, HALF)), lower)
    cov = jnp.concatenate(
        [
            jnp.concatenate([upper, square], axis=1),
            jnp.concatenate([square.T, lower], axis=1),
        ],
        axis=0,
    )
    cov_parts = split_bf16(cov)
    test = live[...]
    mixed = jnp.zeros((FOLDS * COLUMNS, SAMPLES), jnp.float32)
    for part in cov_parts:
        mixed = mixed + jnp.dot(test, part, preferred_element_type=jnp.float32)
    for c in (0, 1):
        mixed_v[c] = mixed[:, c * HALF : (c + 1) * HALF]
    pairs = COLUMNS // 2
    low = iota((pairs, 2 * COLUMNS), 1) < COLUMNS
    for g in range(FOLDS // 4):
        folds = range(4 * g, 4 * g + 4)
        sorted_rows = jnp.concatenate(
            [
                beside(mixed_v, pl.ds(f * COLUMNS + o, pairs, stride=2))
                for f in folds
                for o in (0, 1)
            ],
            axis=0,
        )
        gram = jnp.zeros((WIDE, WIDE), jnp.float32)
        for part in split_bf16(sorted_rows):
            gram = gram + dot_nt(part, test[g * WIDE : (g + 1) * WIDE])
        for f in folds:
            at = f % 4 * COLUMNS
            start = f % 4 // 2 * 2 * COLUMNS
            even, odd = (
                gram[at + o * pairs : at + (o + 1) * pairs, start : start + 2 * COLUMNS]
                for o in (0, 1)
            )
            if f % 2 == 0:
                odd = pltpu.roll(odd, COLUMNS, 1)
            else:
                even = pltpu.roll(even, COLUMNS, 1)
            rows[:, f, :] = jnp.where(low, even, odd)

    eliminate(rows)

    at, pair = iota((pairs, 2 * COLUMNS), 1), iota((pairs, 2 * COLUMNS), 0)
    for f in range(FOLDS):
        left = f % 2 == 0
        found = rows[:, f, :]
        swapped = pltpu.roll(found, COLUMNS, 1)
        column = at if left else at - COLUMNS
        for o in (0, 1):
            keep = (column >= 0) & (column <= 2 * pair + o)
            value = jnp.where(keep, found if left == (o == 0) else swapped, 0.0)
            diag[f % 4 // 2, pl.ds(f * COLUMNS + o, pairs, stride=2), :] = value

    copies = []

    def send(source, target, where):
        copies.append(
            pltpu.make_async_copy(source.at[where], target.at[where], sems.at[len(copies)])
        )
        copies[-1].start()

    for g in range(FOLDS // 4):
        own = slice(g * WIDE, (g + 1) * WIDE)
        inverse = beside(diag, own)
        scale = (inverse * jnp.float32(total**0.5)).astype(jnp.bfloat16)
        for start, width in chunks_of(cols, 768):
            at = slice(start, start + width)
            basis_v[own, at] = jnp.dot(
                scale, scores[own, at], preferred_element_type=jnp.float32
            ).astype(jnp.bfloat16)
            send(basis_v, basis, (pl.ds(g * WIDE, WIDE), pl.ds(start, width)))
        sample_v[own] = jnp.dot(
            inverse * jnp.float32((SAMPLES / total) ** 0.5), beside(mixed_v, own),
            precision=lax.Precision.HIGHEST, preferred_element_type=jnp.float32,
        )
        send(sample_v, sample_basis, (pl.ds(g * WIDE, WIDE),))
    for copy in copies:
        copy.wait()


def spec(space):
    return pl.BlockSpec(memory_space=space)


def grid_total(mine, other):
    devices = lax.axis_size("lat") * lax.axis_size("lon")
    bits = []
    while 2 << len(bits) < devices:
        bits.append(2 << len(bits))
    assert devices == 2 << len(bits)
    steps = [bits[n : n + 2] for n in range(0, len(bits), 2)]
    turn = len(steps) // 2 if len(bits) % 2 == 0 else 0

    def swap(value, even, odd):
        pairs = [(d, d ^ (odd if d % 2 else even)) for d in range(devices)]
        return lax.ppermute(value, AXES, pairs)

    total = mine + swap(other, 1, 1)
    for even, odd in zip(steps, steps[turn:] + steps[:turn]):
        got = [swap(total, *bit) for bit in zip(even, odd)]
        if len(got) == 2:
            last = swap(total, even[0] ^ even[1], odd[0] ^ odd[1])
            total = (total + got[0]) + (got[1] + last)
        else:
            total = total + got[0]
    return total, swap(total, 1, 1)


def on_device(samples, area_weight, ocean_count, omega):
    cols = samples.shape[1]
    total = cols * lax.axis_size("lat") * lax.axis_size("lon")
    half = jax.ShapeDtypeStruct((PACKED, HALF), jnp.float32)
    weighted, mine, other = pl.pallas_call(
        cov_kernel,
        out_shape=(jax.ShapeDtypeStruct((SAMPLES, cols), jnp.bfloat16), half, half),
        in_specs=[spec(pltpu.SMEM), spec(pltpu.HBM), spec(pltpu.HBM)],
        out_specs=(spec(VMEM), spec(VMEM), spec(VMEM)),
        scratch_shapes=[
            VMEM((SAMPLES, cols), jnp.bfloat16),
            VMEM((1, cols), jnp.float32),
            pltpu.SemaphoreType.DMA((8,)),
        ],
        cost_estimate=pl.CostEstimate(
            flops=2 * SAMPLES * SAMPLES * cols, bytes_accessed=4 * SAMPLES * cols, transcendentals=0
        ),
        compiler_params=pltpu.CompilerParams(vmem_limit_bytes=16 << 20),
        name="cov",
    )(
        ocean_count,
        pltpu.with_memory_space_constraint(samples, pltpu.HBM),
        pltpu.with_memory_space_constraint(area_weight, pltpu.HBM),
    )

    mine, other = grid_total(mine, other)

    fold_row = lax.iota(jnp.int32, FOLDS * COLUMNS) // COLUMNS
    fold_col = lax.iota(jnp.int32, SAMPLES) // (SAMPLES // FOLDS)
    keeping = fold_row[:, None] != fold_col[None, :]
    live = jnp.where(keeping, omega, jnp.zeros_like(omega))
    product = jnp.dot(live, weighted, preferred_element_type=jnp.float32)
    scores = product.astype(jnp.bfloat16)

    point_basis, sample_basis = pl.pallas_call(
        lambda *refs: finish_kernel(total, *refs),
        out_shape=(
            jax.ShapeDtypeStruct((FOLDS * COLUMNS, cols), jnp.bfloat16),
            jax.ShapeDtypeStruct((FOLDS * COLUMNS, SAMPLES), jnp.float32),
        ),
        in_specs=[spec(VMEM)] * 4,
        out_specs=(spec(pl.ANY), spec(pl.ANY)),
        scratch_shapes=[
            VMEM((COLUMNS // 2, FOLDS, 2 * COLUMNS), jnp.float32),
            VMEM((2, FOLDS * COLUMNS, WIDE // 2), jnp.float32),
            VMEM((2, FOLDS * COLUMNS, HALF), jnp.float32),
            VMEM((FOLDS * COLUMNS, cols), jnp.bfloat16),
            VMEM((FOLDS * COLUMNS, SAMPLES), jnp.float32),
            pltpu.SemaphoreType.DMA((16,)),
        ],
        compiler_params=pltpu.CompilerParams(vmem_limit_bytes=16 << 20),
        name="finish",
    )(mine, other, live, scores)
    sample_basis = sample_basis.reshape(FOLDS, COLUMNS, SAMPLES)
    return point_basis, sample_basis.transpose(0, 2, 1)


def solution(mesh):
    in_specs = (P(None, AXES), P(AXES), P("lat", "lon"), P())
    out_specs = (P(None, AXES), P())
    return jax.shard_map(
        on_device, mesh=mesh, in_specs=in_specs, out_specs=out_specs, check_vma=False
    )
```

```python
import jax
import jax.numpy as jnp
from jax import lax
from jax.experimental import pallas as pl
from jax.experimental.pallas import tpu as pltpu
from jax.sharding import PartitionSpec as P

SAMPLES = 256
COLUMNS = 64
FOLDS = 8
AXES = ("lat", "lon")
HALF = SAMPLES // 2
QUARTER = HALF // 2
PACKED = 2 * QUARTER + 8
BLOCK = 8
WIDE = 4 * COLUMNS
NT = (((1,), (1,)), ((), ()))
VMEM = pltpu.VMEM
SPLIT = 3


def iota(shape, dim):
    return lax.broadcasted_iota(jnp.int32, shape, dim)


def split_bf16(value):
    parts = []
    for _ in range(SPLIT):
        part = value.astype(jnp.bfloat16)
        parts.append(part)
        value = value - part.astype(jnp.float32)
    return parts


def dot_nt(a, b):
    return lax.dot_general(a, b, NT, preferred_element_type=jnp.float32)


def dot_split(a, b):
    (a_high, a_low), (b_high, b_low) = split_bf16(a)[:2], split_bf16(b)[:2]
    return (jnp.dot(a_high, b_low, preferred_element_type=jnp.float32)
            + jnp.dot(a_low, b_high, preferred_element_type=jnp.float32)
            + jnp.dot(a_high, b_high, preferred_element_type=jnp.float32))


def chunks_of(cols, width):
    return [(start, min(width, cols - start)) for start in range(0, cols, width)]


def cov_kernel(count, samples, area, weighted, mine, other, held, area_v, sems):
    cols = samples.shape[1]
    parts = chunks_of(cols, 1408)
    fetch = pltpu.make_async_copy(area, area_v.at[0], sems.at[len(parts)])
    fetch.start()
    copies = []
    for n, (start, width) in enumerate(parts):
        copies.append(
            pltpu.make_async_copy(
                samples.at[:, pl.ds(start, width)], held.at[:, pl.ds(start, width)], sems.at[n]
            )
        )
        copies[-1].start()
    fetch.wait()
    masked = jnp.where(iota((1, cols), 1) < count[0, 0], area_v[...], 0.0)
    cov = jnp.zeros((SAMPLES, SAMPLES), jnp.float32)
    for copy, (start, width) in zip(copies, parts):
        copy.wait()
        part = held[:, start : start + width].astype(jnp.float32) * masked[:, start : start + width]
        part = part.astype(jnp.bfloat16)
        weighted[:, start : start + width] = part
        cov = cov + dot_nt(part, part)
    row, col = iota((HALF, HALF), 0), iota((HALF, HALF), 1)
    last = cov[HALF:, HALF:]
    diagonal = jnp.sum(jnp.where(row == col, last, 0.0), axis=0, keepdims=True)
    diagonal = jnp.broadcast_to(diagonal, (8, HALF))
    triangles = jnp.where(row >= col, cov[:HALF, :HALF], last)
    square = cov[:HALF, HALF:]
    first = lax.axis_index("lon") % 2 == 0
    for ref, low in ((mine, first), (other, jnp.logical_not(first))):
        ref[:QUARTER] = jnp.where(low, triangles[:QUARTER], triangles[QUARTER:])
        ref[QUARTER:HALF] = jnp.where(low, square[:QUARTER], square[QUARTER:])
        ref[HALF:] = diagonal


def lane(value, i):
    return jnp.broadcast_to(value[:, i : i + 1], value.shape)


def take(value, index):
    return jnp.take_along_axis(value, index, axis=1, mode="promise_in_bounds")


def eliminate(rows):
    at = iota((FOLDS, 2 * COLUMNS), 1)
    even = at < COLUMNS
    column = jnp.where(even, at, at - COLUMNS)
    odd = jnp.where(even, 0, 1)
    for j in range(0, COLUMNS, BLOCK):
        raw = []
        for p in range(j // 2, (j + BLOCK) // 2):
            pair = rows[p]
            swapped = pltpu.roll(pair, COLUMNS, 1)
            raw += [jnp.where(even, pair, swapped), jnp.where(even, swapped, pair)]
        near = range((j + BLOCK) // 2, min(j // 2 + BLOCK, COLUMNS // 2))
        coef = [{r: lane(raw[q], j + r) for r in range(q, BLOCK)} for q in range(BLOCK)]
        pairs = [{p: take(raw[q], odd + 2 * p) for p in near} for q in range(BLOCK)]
        inside = (column >= j) & (column < j + BLOCK)
        pivots = [jnp.where(inside, 0.0, value) for value in raw]
        done = []
        for q in range(BLOCK):
            scale = lax.rsqrt(coef[q][q])
            done.append(jnp.where(column == j + q, scale, pivots[q] * scale))
            for have in (coef[q], pairs[q]):
                for i in have:
                    have[i] = have[i] * scale
            for r in range(q + 1, BLOCK):
                factor = coef[q][r]
                pivots[r] = pivots[r] - factor * done[q]
                for have, used in ((coef, coef[r]), (pairs, pairs[r])):
                    for i in used:
                        used[i] = used[i] - factor * have[q][i]
        for q in range(0, BLOCK, 2):
            rows[(j + q) // 2] = jnp.where(even, done[q], done[q + 1])
        for p in range((j + BLOCK) // 2, COLUMNS // 2):
            value = jnp.where(inside, 0.0, rows[p])
            for q in range(BLOCK):
                factor = pairs[q][p] if p in near else take(done[q], odd + 2 * p)
                value = value - factor * done[q]
            rows[p] = value


def beside(ref, rows):
    return jnp.concatenate([ref[0, rows, :], ref[1, rows, :]], axis=1)


def finish_kernel(total, mine, other, live, scores, basis, sample_basis,
                  rows, diag, mixed_v, basis_v, sample_v, sems):
    cols = scores.shape[1]
    diag[...] = jnp.zeros_like(diag)

    first = lax.axis_index("lon") % 2 == 0
    low = jnp.where(first, mine[...], other[...])
    high = jnp.where(first, other[...], mine[...])
    triangles = jnp.concatenate([low[:QUARTER], high[:QUARTER]], axis=0)
    square = jnp.concatenate([low[QUARTER:HALF], high[QUARTER:HALF]], axis=0)
    row, col = iota((HALF, HALF), 0), iota((HALF, HALF), 1)
    flipped = triangles.T
    upper = jnp.where(row >= col, triangles, flipped)
    lower = jnp.where(row < col, triangles, flipped)
    lower = jnp.where(row == col, jnp.broadcast_to(low[HALF : HALF + 1], (HALF, HALF)), lower)
    cov = jnp.concatenate(
        [
            jnp.concatenate([upper, square], axis=1),
            jnp.concatenate([square.T, lower], axis=1),
        ],
        axis=0,
    )
    cov_parts = split_bf16(cov)
    test = live[...]
    mixed = jnp.zeros((FOLDS * COLUMNS, SAMPLES), jnp.float32)
    for part in cov_parts:
        mixed = mixed + jnp.dot(test, part, preferred_element_type=jnp.float32)
    for c in (0, 1):
        mixed_v[c] = mixed[:, c * HALF : (c + 1) * HALF]
    pairs = COLUMNS // 2
    low = iota((pairs, 2 * COLUMNS), 1) < COLUMNS
    for g in range(FOLDS // 4):
        folds = range(4 * g, 4 * g + 4)
        sorted_rows = jnp.concatenate(
            [
                beside(mixed_v, pl.ds(f * COLUMNS + o, pairs, stride=2))
                for f in folds
                for o in (0, 1)
            ],
            axis=0,
        )
        gram = jnp.zeros((WIDE, WIDE), jnp.float32)
        for part in split_bf16(sorted_rows):
            gram = gram + dot_nt(part, test[g * WIDE : (g + 1) * WIDE])
        for f in folds:
            at = f % 4 * COLUMNS
            start = f % 4 // 2 * 2 * COLUMNS
            even, odd = (
                gram[at + o * pairs : at + (o + 1) * pairs, start : start + 2 * COLUMNS]
                for o in (0, 1)
            )
            if f % 2 == 0:
                odd = pltpu.roll(odd, COLUMNS, 1)
            else:
                even = pltpu.roll(even, COLUMNS, 1)
            rows[:, f, :] = jnp.where(low, even, odd)

    eliminate(rows)

    at, pair = iota((pairs, 2 * COLUMNS), 1), iota((pairs, 2 * COLUMNS), 0)
    for f in range(FOLDS):
        left = f % 2 == 0
        found = rows[:, f, :]
        swapped = pltpu.roll(found, COLUMNS, 1)
        column = at if left else at - COLUMNS
        for o in (0, 1):
            keep = (column >= 0) & (column <= 2 * pair + o)
            value = jnp.where(keep, found if left == (o == 0) else swapped, 0.0)
            diag[f % 4 // 2, pl.ds(f * COLUMNS + o, pairs, stride=2), :] = value

    copies = []

    def send(source, target, where):
        copies.append(
            pltpu.make_async_copy(source.at[where], target.at[where], sems.at[len(copies)])
        )
        copies[-1].start()

    for g in range(FOLDS // 4):
        own = slice(g * WIDE, (g + 1) * WIDE)
        inverse = beside(diag, own)
        scale = (inverse * jnp.float32(total**0.5)).astype(jnp.bfloat16)
        for start, width in chunks_of(cols, 512):
            at = slice(start, start + width)
            basis_v[own, at] = jnp.dot(
                scale, scores[own, at], preferred_element_type=jnp.float32
            ).astype(jnp.bfloat16)
            send(basis_v, basis, (pl.ds(g * WIDE, WIDE), pl.ds(start, width)))
        sample_v[own] = dot_split(
            inverse * jnp.float32((SAMPLES / total) ** 0.5), beside(mixed_v, own)
        )
        send(sample_v, sample_basis, (pl.ds(g * WIDE, WIDE),))
    for copy in copies:
        copy.wait()


def spec(space):
    return pl.BlockSpec(memory_space=space)


def grid_total(mine, other):
    devices = lax.axis_size("lat") * lax.axis_size("lon")
    bits = []
    while 2 << len(bits) < devices:
        bits.append(2 << len(bits))
    assert devices == 2 << len(bits)
    steps = [bits[n : n + 2] for n in range(0, len(bits), 2)]
    turn = len(steps) // 2 if len(bits) % 2 == 0 else 0

    def swap(value, even, odd):
        pairs = [(d, d ^ (odd if d % 2 else even)) for d in range(devices)]
        return lax.ppermute(value, AXES, pairs)

    total = mine + swap(other, 1, 1)
    for even, odd in zip(steps, steps[turn:] + steps[:turn]):
        got = [swap(total, *bit) for bit in zip(even, odd)]
        if len(got) == 2:
            last = swap(total, even[0] ^ even[1], odd[0] ^ odd[1])
            total = (total + got[0]) + (got[1] + last)
        else:
            total = total + got[0]
    return total, swap(total, 1, 1)


def on_device(samples, area_weight, ocean_count, omega):
    cols = samples.shape[1]
    total = cols * lax.axis_size("lat") * lax.axis_size("lon")
    half = jax.ShapeDtypeStruct((PACKED, HALF), jnp.float32)
    weighted, mine, other = pl.pallas_call(
        cov_kernel,
        out_shape=(jax.ShapeDtypeStruct((SAMPLES, cols), jnp.bfloat16), half, half),
        in_specs=[spec(pltpu.SMEM), spec(pltpu.HBM), spec(pltpu.HBM)],
        out_specs=(spec(VMEM), spec(VMEM), spec(VMEM)),
        scratch_shapes=[
            VMEM((SAMPLES, cols), jnp.bfloat16),
            VMEM((1, cols), jnp.float32),
            pltpu.SemaphoreType.DMA((8,)),
        ],
        cost_estimate=pl.CostEstimate(
            flops=2 * SAMPLES * SAMPLES * cols, bytes_accessed=4 * SAMPLES * cols, transcendentals=0
        ),
        compiler_params=pltpu.CompilerParams(vmem_limit_bytes=16 << 20),
        name="cov",
    )(
        ocean_count,
        pltpu.with_memory_space_constraint(samples, pltpu.HBM),
        pltpu.with_memory_space_constraint(area_weight, pltpu.HBM),
    )

    mine, other = grid_total(mine, other)

    fold_row = lax.iota(jnp.int32, FOLDS * COLUMNS) // COLUMNS
    fold_col = lax.iota(jnp.int32, SAMPLES) // (SAMPLES // FOLDS)
    keeping = fold_row[:, None] != fold_col[None, :]
    live = jnp.where(keeping, omega, jnp.zeros_like(omega))
    product = jnp.dot(live, weighted, preferred_element_type=jnp.float32)
    scores = product.astype(jnp.bfloat16)

    point_basis, sample_basis = pl.pallas_call(
        lambda *refs: finish_kernel(total, *refs),
        out_shape=(
            jax.ShapeDtypeStruct((FOLDS * COLUMNS, cols), jnp.bfloat16),
            jax.ShapeDtypeStruct((FOLDS * COLUMNS, SAMPLES), jnp.float32),
        ),
        in_specs=[spec(VMEM)] * 4,
        out_specs=(spec(pl.ANY), spec(pl.ANY)),
        scratch_shapes=[
            VMEM((COLUMNS // 2, FOLDS, 2 * COLUMNS), jnp.float32),
            VMEM((2, FOLDS * COLUMNS, WIDE // 2), jnp.float32),
            VMEM((2, FOLDS * COLUMNS, HALF), jnp.float32),
            VMEM((FOLDS * COLUMNS, cols), jnp.bfloat16),
            VMEM((FOLDS * COLUMNS, SAMPLES), jnp.float32),
            pltpu.SemaphoreType.DMA((16,)),
        ],
        compiler_params=pltpu.CompilerParams(vmem_limit_bytes=16 << 20),
        name="finish",
    )(mine, other, live, scores)
    sample_basis = sample_basis.reshape(FOLDS, COLUMNS, SAMPLES)
    return point_basis, sample_basis.transpose(0, 2, 1)


def solution(mesh):
    in_specs = (P(None, AXES), P(AXES), P("lat", "lon"), P())
    out_specs = (P(None, AXES), P())
    return jax.shard_map(
        on_device, mesh=mesh, in_specs=in_specs, out_specs=out_specs, check_vma=False
    )
```

```python
import jax
import jax.numpy as jnp
from jax import lax
from jax.experimental import pallas as pl
from jax.experimental.pallas import tpu as pltpu
from jax.sharding import PartitionSpec as P

SAMPLES = 256
COLUMNS = 64
FOLDS = 8
AXES = ("lat", "lon")
HALF = SAMPLES // 2
QUARTER = HALF // 2
PACKED = 2 * QUARTER + 8
BLOCK = 8
WIDE = 4 * COLUMNS
NT = (((1,), (1,)), ((), ()))
VMEM = pltpu.VMEM
SPLIT = 3


def iota(shape, dim):
    return lax.broadcasted_iota(jnp.int32, shape, dim)


def split_bf16(value):
    parts = []
    for _ in range(SPLIT):
        part = value.astype(jnp.bfloat16)
        parts.append(part)
        value = value - part.astype(jnp.float32)
    return parts


def dot_nt(a, b):
    return lax.dot_general(a, b, NT, preferred_element_type=jnp.float32)


def dot_split(a, b):
    (a_high, a_low), (b_high, b_low) = split_bf16(a)[:2], split_bf16(b)[:2]
    return (jnp.dot(a_high, b_low, preferred_element_type=jnp.float32)
            + jnp.dot(a_low, b_high, preferred_element_type=jnp.float32)
            + jnp.dot(a_high, b_high, preferred_element_type=jnp.float32))


def chunks_of(cols, width):
    return [(start, min(width, cols - start)) for start in range(0, cols, width)]


def cov_kernel(count, samples, area, weighted, mine, other, held, area_v, sems):
    cols = samples.shape[1]
    parts = [(0, 768), (768, cols - 768)]
    fetch = pltpu.make_async_copy(area, area_v.at[0], sems.at[len(parts)])
    fetch.start()
    copies = []
    for n, (start, width) in enumerate(parts):
        copies.append(
            pltpu.make_async_copy(
                samples.at[:, pl.ds(start, width)], held.at[:, pl.ds(start, width)], sems.at[n]
            )
        )
        copies[-1].start()
    fetch.wait()
    masked = jnp.where(iota((1, cols), 1) < count[0, 0], area_v[...], 0.0)
    cov = jnp.zeros((SAMPLES, SAMPLES), jnp.float32)
    for copy, (start, width) in zip(copies, parts):
        copy.wait()
        part = held[:, start : start + width].astype(jnp.float32) * masked[:, start : start + width]
        part = part.astype(jnp.bfloat16)
        weighted[:, start : start + width] = part
        cov = cov + dot_nt(part, part)
    row, col = iota((HALF, HALF), 0), iota((HALF, HALF), 1)
    last = cov[HALF:, HALF:]
    diagonal = jnp.sum(jnp.where(row == col, last, 0.0), axis=0, keepdims=True)
    diagonal = jnp.broadcast_to(diagonal, (8, HALF))
    triangles = jnp.where(row >= col, cov[:HALF, :HALF], last)
    square = cov[:HALF, HALF:]
    first = lax.axis_index("lon") % 2 == 0
    for ref, low in ((mine, first), (other, jnp.logical_not(first))):
        ref[:QUARTER] = jnp.where(low, triangles[:QUARTER], triangles[QUARTER:])
        ref[QUARTER:HALF] = jnp.where(low, square[:QUARTER], square[QUARTER:])
        ref[HALF:] = diagonal


def lane(value, i):
    return jnp.broadcast_to(value[:, i : i + 1], value.shape)


def take(value, index):
    return jnp.take_along_axis(value, index, axis=1, mode="promise_in_bounds")


def eliminate(rows):
    at = iota((FOLDS, 2 * COLUMNS), 1)
    even = at < COLUMNS
    column = jnp.where(even, at, at - COLUMNS)
    odd = jnp.where(even, 0, 1)
    for j in range(0, COLUMNS, BLOCK):
        raw = []
        for p in range(j // 2, (j + BLOCK) // 2):
            pair = rows[p]
            swapped = pltpu.roll(pair, COLUMNS, 1)
            raw += [jnp.where(even, pair, swapped), jnp.where(even, swapped, pair)]
        near = range((j + BLOCK) // 2, min(j // 2 + BLOCK, COLUMNS // 2))
        coef = [{r: lane(raw[q], j + r) for r in range(q, BLOCK)} for q in range(BLOCK)]
        pairs = [{p: take(raw[q], odd + 2 * p) for p in near} for q in range(BLOCK)]
        inside = (column >= j) & (column < j + BLOCK)
        pivots = [jnp.where(inside, 0.0, value) for value in raw]
        done = []
        for q in range(BLOCK):
            scale = lax.rsqrt(coef[q][q])
            done.append(jnp.where(column == j + q, scale, pivots[q] * scale))
            for have in (coef[q], pairs[q]):
                for i in have:
                    have[i] = have[i] * scale
            for r in range(q + 1, BLOCK):
                factor = coef[q][r]
                pivots[r] = pivots[r] - factor * done[q]
                for have, used in ((coef, coef[r]), (pairs, pairs[r])):
                    for i in used:
                        used[i] = used[i] - factor * have[q][i]
        for q in range(0, BLOCK, 2):
            rows[(j + q) // 2] = jnp.where(even, done[q], done[q + 1])
        for p in range((j + BLOCK) // 2, COLUMNS // 2):
            value = jnp.where(inside, 0.0, rows[p])
            for q in range(BLOCK):
                factor = pairs[q][p] if p in near else take(done[q], odd + 2 * p)
                value = value - factor * done[q]
            rows[p] = value


def beside(ref, rows):
    return jnp.concatenate([ref[0, rows, :], ref[1, rows, :]], axis=1)


def finish_kernel(total, mine, other, live, scores, basis, sample_basis,
                  rows, diag, mixed_v, basis_v, sample_v, sems):
    cols = scores.shape[1]
    diag[...] = jnp.zeros_like(diag)

    first = lax.axis_index("lon") % 2 == 0
    low = jnp.where(first, mine[...], other[...])
    high = jnp.where(first, other[...], mine[...])
    triangles = jnp.concatenate([low[:QUARTER], high[:QUARTER]], axis=0)
    square = jnp.concatenate([low[QUARTER:HALF], high[QUARTER:HALF]], axis=0)
    row, col = iota((HALF, HALF), 0), iota((HALF, HALF), 1)
    flipped = triangles.T
    upper = jnp.where(row >= col, triangles, flipped)
    lower = jnp.where(row < col, triangles, flipped)
    lower = jnp.where(row == col, jnp.broadcast_to(low[HALF : HALF + 1], (HALF, HALF)), lower)
    cov = jnp.concatenate(
        [
            jnp.concatenate([upper, square], axis=1),
            jnp.concatenate([square.T, lower], axis=1),
        ],
        axis=0,
    )
    cov_parts = split_bf16(cov)
    test = live[...]
    mixed = jnp.zeros((FOLDS * COLUMNS, SAMPLES), jnp.float32)
    for part in cov_parts:
        mixed = mixed + jnp.dot(test, part, preferred_element_type=jnp.float32)
    for c in (0, 1):
        mixed_v[c] = mixed[:, c * HALF : (c + 1) * HALF]
    pairs = COLUMNS // 2
    low = iota((pairs, 2 * COLUMNS), 1) < COLUMNS
    for g in range(FOLDS // 4):
        folds = range(4 * g, 4 * g + 4)
        sorted_rows = jnp.concatenate(
            [
                beside(mixed_v, pl.ds(f * COLUMNS + o, pairs, stride=2))
                for f in folds
                for o in (0, 1)
            ],
            axis=0,
        )
        gram = jnp.zeros((WIDE, WIDE), jnp.float32)
        for part in split_bf16(sorted_rows):
            gram = gram + dot_nt(part, test[g * WIDE : (g + 1) * WIDE])
        for f in folds:
            at = f % 4 * COLUMNS
            start = f % 4 // 2 * 2 * COLUMNS
            even, odd = (
                gram[at + o * pairs : at + (o + 1) * pairs, start : start + 2 * COLUMNS]
                for o in (0, 1)
            )
            if f % 2 == 0:
                odd = pltpu.roll(odd, COLUMNS, 1)
            else:
                even = pltpu.roll(even, COLUMNS, 1)
            rows[:, f, :] = jnp.where(low, even, odd)

    eliminate(rows)

    at, pair = iota((pairs, 2 * COLUMNS), 1), iota((pairs, 2 * COLUMNS), 0)
    for f in range(FOLDS):
        left = f % 2 == 0
        found = rows[:, f, :]
        swapped = pltpu.roll(found, COLUMNS, 1)
        column = at if left else at - COLUMNS
        for o in (0, 1):
            keep = (column >= 0) & (column <= 2 * pair + o)
            value = jnp.where(keep, found if left == (o == 0) else swapped, 0.0)
            diag[f % 4 // 2, pl.ds(f * COLUMNS + o, pairs, stride=2), :] = value

    copies = []

    def send(source, target, where):
        copies.append(
            pltpu.make_async_copy(source.at[where], target.at[where], sems.at[len(copies)])
        )
        copies[-1].start()

    for g in range(FOLDS // 4):
        own = slice(g * WIDE, (g + 1) * WIDE)
        inverse = beside(diag, own)
        scale = (inverse * jnp.float32(total**0.5)).astype(jnp.bfloat16)
        for start, width in chunks_of(cols, 512):
            at = slice(start, start + width)
            basis_v[own, at] = jnp.dot(
                scale, scores[own, at], preferred_element_type=jnp.float32
            ).astype(jnp.bfloat16)
            send(basis_v, basis, (pl.ds(g * WIDE, WIDE), pl.ds(start, width)))
        sample_v[own] = dot_split(
            inverse * jnp.float32((SAMPLES / total) ** 0.5), beside(mixed_v, own)
        )
        send(sample_v, sample_basis, (pl.ds(g * WIDE, WIDE),))
    for copy in copies:
        copy.wait()


def spec(space):
    return pl.BlockSpec(memory_space=space)


def grid_total(mine, other, scores):
    devices = lax.axis_size("lat") * lax.axis_size("lon")
    bits = []
    while 2 << len(bits) < devices:
        bits.append(2 << len(bits))
    assert devices == 2 << len(bits)
    steps = [bits[n : n + 2] for n in range(0, len(bits), 2)]
    turn = len(steps) // 2 if len(bits) % 2 == 0 else 0

    def swap(value, even, odd):
        pairs = [(d, d ^ (odd if d % 2 else even)) for d in range(devices)]
        return lax.ppermute(value, AXES, pairs)

    total = mine + swap(other, 1, 1)
    for even, odd in zip(steps, steps[turn:] + steps[:turn]):
        got = [swap(total, *bit) for bit in zip(even, odd)]
        if len(got) == 2:
            last = swap(total, even[0] ^ even[1], odd[0] ^ odd[1])
            total = (total + got[0]) + (got[1] + last)
        else:
            total = total + got[0]
    total, scores = lax.optimization_barrier((total, scores))
    return total, swap(total, 1, 1), scores


def on_device(samples, area_weight, ocean_count, omega):
    cols = samples.shape[1]
    total = cols * lax.axis_size("lat") * lax.axis_size("lon")
    half = jax.ShapeDtypeStruct((PACKED, HALF), jnp.float32)
    weighted, mine, other = pl.pallas_call(
        cov_kernel,
        out_shape=(jax.ShapeDtypeStruct((SAMPLES, cols), jnp.bfloat16), half, half),
        in_specs=[spec(pltpu.SMEM), spec(pltpu.HBM), spec(pltpu.HBM)],
        out_specs=(spec(VMEM), spec(VMEM), spec(VMEM)),
        scratch_shapes=[
            VMEM((SAMPLES, cols), jnp.bfloat16),
            VMEM((1, cols), jnp.float32),
            pltpu.SemaphoreType.DMA((8,)),
        ],
        cost_estimate=pl.CostEstimate(
            flops=2 * SAMPLES * SAMPLES * cols, bytes_accessed=4 * SAMPLES * cols, transcendentals=0
        ),
        compiler_params=pltpu.CompilerParams(vmem_limit_bytes=16 << 20),
        name="cov",
    )(
        ocean_count,
        pltpu.with_memory_space_constraint(samples, pltpu.HBM),
        pltpu.with_memory_space_constraint(area_weight, pltpu.HBM),
    )

    fold_row = lax.iota(jnp.int32, FOLDS * COLUMNS) // COLUMNS
    fold_col = lax.iota(jnp.int32, SAMPLES) // (SAMPLES // FOLDS)
    keeping = fold_row[:, None] != fold_col[None, :]
    live = jnp.where(keeping, omega, jnp.zeros_like(omega))
    product = jnp.dot(live, weighted, preferred_element_type=jnp.float32)
    scores = product.astype(jnp.bfloat16)
    mine, other, scores = grid_total(mine, other, scores)

    point_basis, sample_basis = pl.pallas_call(
        lambda *refs: finish_kernel(total, *refs),
        out_shape=(
            jax.ShapeDtypeStruct((FOLDS * COLUMNS, cols), jnp.bfloat16),
            jax.ShapeDtypeStruct((FOLDS * COLUMNS, SAMPLES), jnp.float32),
        ),
        in_specs=[spec(VMEM)] * 4,
        out_specs=(spec(pl.ANY), spec(pl.ANY)),
        scratch_shapes=[
            VMEM((COLUMNS // 2, FOLDS, 2 * COLUMNS), jnp.float32),
            VMEM((2, FOLDS * COLUMNS, WIDE // 2), jnp.float32),
            VMEM((2, FOLDS * COLUMNS, HALF), jnp.float32),
            VMEM((FOLDS * COLUMNS, cols), jnp.bfloat16),
            VMEM((FOLDS * COLUMNS, SAMPLES), jnp.float32),
            pltpu.SemaphoreType.DMA((16,)),
        ],
        compiler_params=pltpu.CompilerParams(vmem_limit_bytes=16 << 20),
        name="finish",
    )(mine, other, live, scores)
    sample_basis = sample_basis.reshape(FOLDS, COLUMNS, SAMPLES)
    return point_basis, sample_basis.transpose(0, 2, 1)


def solution(mesh):
    in_specs = (P(None, AXES), P(AXES), P("lat", "lon"), P())
    out_specs = (P(None, AXES), P())
    return jax.shard_map(
        on_device, mesh=mesh, in_specs=in_specs, out_specs=out_specs, check_vma=False
    )
```

```python
import jax
import jax.numpy as jnp
from jax import lax
from jax.experimental import pallas as pl
from jax.experimental.pallas import tpu as pltpu
from jax.sharding import PartitionSpec as P

SAMPLES = 256
COLUMNS = 64
FOLDS = 8
AXES = ("lat", "lon")
HALF = SAMPLES // 2
QUARTER = HALF // 2
PACKED = 2 * QUARTER + 8
BLOCK = 8
WIDE = 4 * COLUMNS
NT = (((1,), (1,)), ((), ()))
VMEM = pltpu.VMEM
SPLIT = 3
EARLY = 512


def iota(shape, dim):
    return lax.broadcasted_iota(jnp.int32, shape, dim)


def split_bf16(value):
    parts = []
    for _ in range(SPLIT):
        part = value.astype(jnp.bfloat16)
        parts.append(part)
        value = value - part.astype(jnp.float32)
    return parts


def dot_nt(a, b):
    return lax.dot_general(a, b, NT, preferred_element_type=jnp.float32)


def dot_split(a, b):
    (a_high, a_low), (b_high, b_low) = split_bf16(a)[:2], split_bf16(b)[:2]
    return (jnp.dot(a_high, b_low, preferred_element_type=jnp.float32)
            + jnp.dot(a_low, b_high, preferred_element_type=jnp.float32)
            + jnp.dot(a_high, b_high, preferred_element_type=jnp.float32))


def chunks_of(cols, width):
    return [(start, min(width, cols - start)) for start in range(0, cols, width)]


def cov_kernel(count, samples, area, weighted, mine, other, held, area_v, sems):
    cols = samples.shape[1]
    parts = chunks_of(cols, 1408)
    fetch = pltpu.make_async_copy(area, area_v.at[0], sems.at[len(parts)])
    fetch.start()
    copies = []
    for n, (start, width) in enumerate(parts):
        copies.append(
            pltpu.make_async_copy(
                samples.at[:, pl.ds(start, width)], held.at[:, pl.ds(start, width)], sems.at[n]
            )
        )
        copies[-1].start()
    fetch.wait()
    masked = jnp.where(iota((1, cols), 1) < count[0, 0], area_v[...], 0.0)
    cov = jnp.zeros((SAMPLES, SAMPLES), jnp.float32)
    for copy, (start, width) in zip(copies, parts):
        copy.wait()
        part = held[:, start : start + width].astype(jnp.float32) * masked[:, start : start + width]
        part = part.astype(jnp.bfloat16)
        weighted[:, start : start + width] = part
        cov = cov + dot_nt(part, part)
    row, col = iota((HALF, HALF), 0), iota((HALF, HALF), 1)
    last = cov[HALF:, HALF:]
    diagonal = jnp.sum(jnp.where(row == col, last, 0.0), axis=0, keepdims=True)
    diagonal = jnp.broadcast_to(diagonal, (8, HALF))
    triangles = jnp.where(row >= col, cov[:HALF, :HALF], last)
    square = cov[:HALF, HALF:]
    first = lax.axis_index("lon") % 2 == 0
    for ref, low in ((mine, first), (other, jnp.logical_not(first))):
        ref[:QUARTER] = jnp.where(low, triangles[:QUARTER], triangles[QUARTER:])
        ref[QUARTER:HALF] = jnp.where(low, square[:QUARTER], square[QUARTER:])
        ref[HALF:] = diagonal


def lane(value, i):
    return jnp.broadcast_to(value[:, i : i + 1], value.shape)


def take(value, index):
    return jnp.take_along_axis(value, index, axis=1, mode="promise_in_bounds")


def eliminate(rows, between):
    at = iota((FOLDS, 2 * COLUMNS), 1)
    even = at < COLUMNS
    column = jnp.where(even, at, at - COLUMNS)
    odd = jnp.where(even, 0, 1)
    for j in range(0, COLUMNS, BLOCK):
        raw = []
        for p in range(j // 2, (j + BLOCK) // 2):
            pair = rows[p]
            swapped = pltpu.roll(pair, COLUMNS, 1)
            raw += [jnp.where(even, pair, swapped), jnp.where(even, swapped, pair)]
        near = range((j + BLOCK) // 2, min(j // 2 + BLOCK, COLUMNS // 2))
        coef = [{r: lane(raw[q], j + r) for r in range(q, BLOCK)} for q in range(BLOCK)]
        pairs = [{p: take(raw[q], odd + 2 * p) for p in near} for q in range(BLOCK)]
        inside = (column >= j) & (column < j + BLOCK)
        pivots = [jnp.where(inside, 0.0, value) for value in raw]
        done = []
        for q in range(BLOCK):
            scale = lax.rsqrt(coef[q][q])
            done.append(jnp.where(column == j + q, scale, pivots[q] * scale))
            for have in (coef[q], pairs[q]):
                for i in have:
                    have[i] = have[i] * scale
            for r in range(q + 1, BLOCK):
                factor = coef[q][r]
                pivots[r] = pivots[r] - factor * done[q]
                for have, used in ((coef, coef[r]), (pairs, pairs[r])):
                    for i in used:
                        used[i] = used[i] - factor * have[q][i]
        for q in range(0, BLOCK, 2):
            rows[(j + q) // 2] = jnp.where(even, done[q], done[q + 1])
        for p in range((j + BLOCK) // 2, COLUMNS // 2):
            value = jnp.where(inside, 0.0, rows[p])
            for q in range(BLOCK):
                factor = pairs[q][p] if p in near else take(done[q], odd + 2 * p)
                value = value - factor * done[q]
            rows[p] = value
        between(j + BLOCK)


def beside(ref, rows):
    return jnp.concatenate([ref[0, rows, :], ref[1, rows, :]], axis=1)


def finish_kernel(total, mine, other, live, scores, basis, sample_basis,
                  rows, diag_low, diag, mixed_v, basis_v, sample_v, sems):
    cols = scores.shape[1]
    diag_low[...] = jnp.zeros_like(diag_low)
    diag[...] = jnp.zeros_like(diag)

    first = lax.axis_index("lon") % 2 == 0
    low = jnp.where(first, mine[...], other[...])
    high = jnp.where(first, other[...], mine[...])
    triangles = jnp.concatenate([low[:QUARTER], high[:QUARTER]], axis=0)
    square = jnp.concatenate([low[QUARTER:HALF], high[QUARTER:HALF]], axis=0)
    row, col = iota((HALF, HALF), 0), iota((HALF, HALF), 1)
    flipped = triangles.T
    upper = jnp.where(row >= col, triangles, flipped)
    lower = jnp.where(row < col, triangles, flipped)
    lower = jnp.where(row == col, jnp.broadcast_to(low[HALF : HALF + 1], (HALF, HALF)), lower)
    cov = jnp.concatenate(
        [
            jnp.concatenate([upper, square], axis=1),
            jnp.concatenate([square.T, lower], axis=1),
        ],
        axis=0,
    )
    cov_parts = split_bf16(cov)
    test = live[...]
    mixed = jnp.zeros((FOLDS * COLUMNS, SAMPLES), jnp.float32)
    for part in cov_parts:
        mixed = mixed + jnp.dot(test, part, preferred_element_type=jnp.float32)
    for c in (0, 1):
        mixed_v[c] = mixed[:, c * HALF : (c + 1) * HALF]
    pairs = COLUMNS // 2
    low = iota((pairs, 2 * COLUMNS), 1) < COLUMNS
    for g in range(FOLDS // 4):
        folds = range(4 * g, 4 * g + 4)
        sorted_rows = jnp.concatenate(
            [
                beside(mixed_v, pl.ds(f * COLUMNS + o, pairs, stride=2))
                for f in folds
                for o in (0, 1)
            ],
            axis=0,
        )
        gram = jnp.zeros((WIDE, WIDE), jnp.float32)
        for part in split_bf16(sorted_rows):
            gram = gram + dot_nt(part, test[g * WIDE : (g + 1) * WIDE])
        for f in folds:
            at = f % 4 * COLUMNS
            start = f % 4 // 2 * 2 * COLUMNS
            even, odd = (
                gram[at + o * pairs : at + (o + 1) * pairs, start : start + 2 * COLUMNS]
                for o in (0, 1)
            )
            if f % 2 == 0:
                odd = pltpu.roll(odd, COLUMNS, 1)
            else:
                even = pltpu.roll(even, COLUMNS, 1)
            rows[:, f, :] = jnp.where(low, even, odd)

    half = COLUMNS // 2
    lanes, pair = iota((half // 2, 2 * COLUMNS), 1), iota((half // 2, 2 * COLUMNS), 0)
    point_factor = jnp.float32(total**0.5)
    sample_factor = jnp.float32((SAMPLES / total) ** 0.5)

    def extract(target, upper, width):
        for f in range(FOLDS):
            tile, start = divmod(f * width % WIDE, 2 * COLUMNS)
            found = rows[upper * half // 2 : (upper + 1) * half // 2, f, :]
            column = lanes - start
            for o in (0, 1):
                shift = (start - o * COLUMNS) % (2 * COLUMNS)
                moved = pltpu.roll(found, shift, 1) if shift else found
                keep = (column >= 0) & (column <= 2 * pair + o + upper * half)
                target[tile, pl.ds(f * half + o, half // 2, stride=2), :] = jnp.where(
                    keep, moved, 0.0
                )

    def lower_rows(ref, at):
        return jnp.concatenate(
            [ref[f * COLUMNS : f * COLUMNS + half, at] for f in range(FOLDS)], axis=0
        )

    early = {}

    def basis_early(at):
        found = jnp.dot(
            early["scale"], lower_rows(scores, at), preferred_element_type=jnp.float32
        ).astype(jnp.bfloat16)
        for f in range(FOLDS):
            basis_v[f * COLUMNS : f * COLUMNS + half, at] = found[f * half : (f + 1) * half]

    def sample_early():
        mixed_low = jnp.concatenate(
            [beside(mixed_v, slice(f * COLUMNS, f * COLUMNS + half)) for f in range(FOLDS)], axis=0
        )
        found = dot_split(early["inverse"] * sample_factor, mixed_low)
        for f in range(FOLDS):
            sample_v[f * COLUMNS : f * COLUMNS + half] = found[f * half : (f + 1) * half]

    work = [sample_early]
    for start, width in chunks_of(cols, EARLY):
        work.append(lambda at=slice(start, start + width): basis_early(at))

    def between(ready):
        if ready == half:
            extract(diag_low, 0, half)
            early["inverse"] = beside(diag_low, slice(None))
            early["scale"] = (early["inverse"] * point_factor).astype(jnp.bfloat16)
        elif ready > half:
            left = (COLUMNS - ready) // BLOCK + 1
            for _ in range(-(-len(work) // left)):
                work.pop(0)()

    eliminate(rows, between)

    extract(diag, 1, COLUMNS)
    copies = []

    def send(source, target, where):
        copies.append(
            pltpu.make_async_copy(source.at[where], target.at[where], sems.at[len(copies)])
        )
        copies[-1].start()

    for g in range(FOLDS // 4):
        own = slice(g * WIDE, (g + 1) * WIDE)
        inverse = beside(diag, slice(g * WIDE // 2, (g + 1) * WIDE // 2))
        scale = (inverse * point_factor).astype(jnp.bfloat16)
        for start, width in chunks_of(cols, 768):
            at = slice(start, start + width)
            found = jnp.dot(
                scale, scores[own, at], preferred_element_type=jnp.float32
            ).astype(jnp.bfloat16)
            for n in range(4):
                row = g * WIDE + n * COLUMNS + half
                basis_v[row : row + half, at] = found[n * half : (n + 1) * half]
            send(basis_v, basis, (pl.ds(g * WIDE, WIDE), pl.ds(start, width)))
        found = dot_split(inverse * sample_factor, beside(mixed_v, own))
        for n in range(4):
            row = g * WIDE + n * COLUMNS + half
            sample_v[row : row + half] = found[n * half : (n + 1) * half]
        send(sample_v, sample_basis, (pl.ds(g * WIDE, WIDE),))
    for copy in copies:
        copy.wait()


def spec(space):
    return pl.BlockSpec(memory_space=space)


def grid_total(mine, other):
    devices = lax.axis_size("lat") * lax.axis_size("lon")
    bits = []
    while 2 << len(bits) < devices:
        bits.append(2 << len(bits))
    assert devices == 2 << len(bits)
    steps = [bits[n : n + 2] for n in range(0, len(bits), 2)]
    turn = len(steps) // 2 if len(bits) % 2 == 0 else 0

    def swap(value, even, odd):
        pairs = [(d, d ^ (odd if d % 2 else even)) for d in range(devices)]
        return lax.ppermute(value, AXES, pairs)

    total = mine + swap(other, 1, 1)
    for even, odd in zip(steps, steps[turn:] + steps[:turn]):
        got = [swap(total, *bit) for bit in zip(even, odd)]
        if len(got) == 2:
            last = swap(total, even[0] ^ even[1], odd[0] ^ odd[1])
            total = (total + got[0]) + (got[1] + last)
        else:
            total = total + got[0]
    return total, swap(total, 1, 1)


def on_device(samples, area_weight, ocean_count, omega):
    cols = samples.shape[1]
    total = cols * lax.axis_size("lat") * lax.axis_size("lon")
    half = jax.ShapeDtypeStruct((PACKED, HALF), jnp.float32)
    weighted, mine, other = pl.pallas_call(
        cov_kernel,
        out_shape=(jax.ShapeDtypeStruct((SAMPLES, cols), jnp.bfloat16), half, half),
        in_specs=[spec(pltpu.SMEM), spec(pltpu.HBM), spec(pltpu.HBM)],
        out_specs=(spec(VMEM), spec(VMEM), spec(VMEM)),
        scratch_shapes=[
            VMEM((SAMPLES, cols), jnp.bfloat16),
            VMEM((1, cols), jnp.float32),
            pltpu.SemaphoreType.DMA((8,)),
        ],
        cost_estimate=pl.CostEstimate(
            flops=2 * SAMPLES * SAMPLES * cols, bytes_accessed=4 * SAMPLES * cols, transcendentals=0
        ),
        compiler_params=pltpu.CompilerParams(vmem_limit_bytes=16 << 20),
        name="cov",
    )(
        ocean_count,
        pltpu.with_memory_space_constraint(samples, pltpu.HBM),
        pltpu.with_memory_space_constraint(area_weight, pltpu.HBM),
    )

    mine, other = grid_total(mine, other)

    fold_row = lax.iota(jnp.int32, FOLDS * COLUMNS) // COLUMNS
    fold_col = lax.iota(jnp.int32, SAMPLES) // (SAMPLES // FOLDS)
    keeping = fold_row[:, None] != fold_col[None, :]
    live = jnp.where(keeping, omega, jnp.zeros_like(omega))
    product = jnp.dot(live, weighted, preferred_element_type=jnp.float32)
    scores = product.astype(jnp.bfloat16)

    point_basis, sample_basis = pl.pallas_call(
        lambda *refs: finish_kernel(total, *refs),
        out_shape=(
            jax.ShapeDtypeStruct((FOLDS * COLUMNS, cols), jnp.bfloat16),
            jax.ShapeDtypeStruct((FOLDS * COLUMNS, SAMPLES), jnp.float32),
        ),
        in_specs=[spec(VMEM)] * 4,
        out_specs=(spec(pl.ANY), spec(pl.ANY)),
        scratch_shapes=[
            VMEM((COLUMNS // 2, FOLDS, 2 * COLUMNS), jnp.float32),
            VMEM((2, FOLDS * COLUMNS // 2, WIDE // 2), jnp.float32),
            VMEM((2, FOLDS * COLUMNS // 2, WIDE // 2), jnp.float32),
            VMEM((2, FOLDS * COLUMNS, HALF), jnp.float32),
            VMEM((FOLDS * COLUMNS, cols), jnp.bfloat16),
            VMEM((FOLDS * COLUMNS, SAMPLES), jnp.float32),
            pltpu.SemaphoreType.DMA((16,)),
        ],
        compiler_params=pltpu.CompilerParams(vmem_limit_bytes=16 << 20),
        name="finish",
    )(mine, other, live, scores)
    sample_basis = sample_basis.reshape(FOLDS, COLUMNS, SAMPLES)
    return point_basis, sample_basis.transpose(0, 2, 1)


def solution(mesh):
    in_specs = (P(None, AXES), P(AXES), P("lat", "lon"), P())
    out_specs = (P(None, AXES), P())
    return jax.shard_map(
        on_device, mesh=mesh, in_specs=in_specs, out_specs=out_specs, check_vma=False
    )
```
